256 devices in a mesh: ctx: 16 (over z_lo, y, core), heads: 16 (over z_hi, x).
Axes of the slice: x: 4, y: 4, z: 8 (z_hi: 4, z_lo: 2; z = z_hi * 2 + z_lo), core: 2. Of those that a mesh axis runs over, the one named last changes fastest.
Arguments:
- queries: bfloat16 [4096, 8192], P('ctx', 'heads'), may hold values from -48 to 48
- out_grad: bfloat16 [4096, 8192], P('ctx', 'heads'), may hold values from -48 to 48
- attn_out: bfloat16 [4096, 8192], P('ctx', 'heads'), may hold values from -6 to 6
- img_keys: bfloat16 [2048, 1024], P('ctx'), may hold values from -6 to 6
- img_values: bfloat16 [2048, 1024], P('ctx'), may hold values from -6 to 6
- key_weight: bfloat16 [8192, 1024], P('heads'), may hold values from -0.0625 to 0.0625
- value_weight: bfloat16 [8192, 1024], P('heads'), may hold values from -0.0625 to 0.0625
- proj_weight: bfloat16 [7680, 8192], P('heads'), may hold values from -0.0625 to 0.0625
- block_order: int32 [32], replicated, may hold values from 0 to 31, each once
- owner_counts: int32 [16], replicated, may hold values from 1 to 4, 32 in all
Outputs:
- d_query: bfloat16 [4096, 8192], P('ctx', 'heads')
- d_vision: bfloat16 [4096, 7680], P('ctx', 'heads')
The draws below stay inside these ranges and needn't reach their ends.
Inputs may be any that keep to these rules, and one draw needn't show every extreme that they name: `block_order`: each of the 32 blocks appears once. `owner_counts`: the counts sum to 32; one owner has exactly 4.
All inputs are finite; a program needn't handle non-finite values.
Results may differ from the reference program's by a relative error of at most 0.015.
Values may be sent and summed in bfloat16 or wider, within the bound.
No kernel may reach another device: no remote copies, remote signals or barrier semaphores. Data moves between devices by JAX's collectives and lax.ppermute only.
A program may use at most 64 MiB of HBM per device.

```python
import math
import jax
import jax.numpy as jnp
import numpy as np
from jax import lax

DM = 8192
VW = 7680
QH = 64
KVH = 8
HD = 128
BR = 64
OWNERS = 16
NB = 32
CAP = 4
IMG = 2048
TEXT = 4096


def raw_keys(key):
    return jax.random.truncated_normal(jax.random.fold_in(key, 5), -6.0, 6.0, (IMG, KVH * HD), jnp.float32)


def draw_img_keys(key, part):
    return raw_keys(key).astype(jnp.bfloat16)


def draw_queries(key, part):
    return jax.random.truncated_normal(jax.random.fold_in(key, 6), -6.0, 6.0, (TEXT, QH * HD), jnp.float32).astype(jnp.bfloat16)


def shard_levels(own_key, dims, cuts, low, largest):
    def one(axis_at, shards_of):
        heights = jax.random.uniform(jax.random.fold_in(jax.random.fold_in(own_key, 6), axis_at), (shards_of,), jnp.float32, low / len(cuts), largest / len(cuts))
        return jnp.repeat(jnp.exp(heights), dims[axis_at] // shards_of).reshape((-1,) + (1,) * (len(dims) - axis_at - 1))

    factor_of = one(*cuts[0])
    for cut in cuts[1:]:
        factor_of = factor_of * one(*cut)
    return factor_of


def split_up(count, total, most, skew):
    portions = [(1 << 20) // math.isqrt(standing ** skew) + 1 for standing in range(2, count + 1)]
    spare, given = total - most - (count - 1), [1] * (count - 1)
    while spare > 0:
        candidates = [i for i in range(count - 1) if given[i] < most]
        pool, remaining = sum([portions[i] for i in candidates]), spare
        for i in candidates:
            addition = min(most - given[i], max(1, remaining * portions[i] // pool), spare)
            given[i] = given[i] + addition
            spare = spare - addition
    return np.array([most] + given)


def uneven_parts(key, number_of, total, most, slope):
    if number_of == 2:
        one = jax.random.randint(key, (), max(1, total - most), min(most, total - 1) + 1)
        return jnp.stack([one, total - one])
    sizes = jnp.asarray(split_up(number_of, total, most, slope), jnp.int32)
    twos = (number_of - 1) // 2
    giver, taker = sizes[1:1 + 2 * twos:2], sizes[2:2 + 2 * twos:2]
    room = jnp.minimum(giver - 1, most - taker)
    moved = jax.random.randint(jax.random.fold_in(key, 1), (twos,), 0, 1 << 20) % (room + 1)
    sizes = sizes.at[1:1 + 2 * twos:2].set(giver - moved).at[2:2 + 2 * twos:2].set(taker + moved)
    return sizes[jax.random.permutation(jax.random.fold_in(key, 2), number_of)]


def centred(key, extent, width, most, pieces=(), held_as=jnp.bfloat16):
    entries = width * jax.random.normal(key, extent, jnp.float32)
    if pieces:
        entries = entries * shard_levels(key, extent, pieces, -0.22, 0.18)
    return jnp.clip(entries, -most, most).astype(held_as)


def setup_inputs(seed: int = 0) -> dict:
    keys = jax.random.split(jax.random.key(seed), 11)
    return {
        "queries": draw_queries(jax.random.fold_in(keys[10], 71), 0),
        "out_grad": centred(keys[1], (TEXT, QH * HD), 8.0, 48.0, ((0, 16), (1, 16))),
        "attn_out": centred(keys[2], (TEXT, QH * HD), 1.0, 6.0, ((0, 16), (1, 16))),
        "img_keys": draw_img_keys(jax.random.fold_in(keys[10], 71), 0),
        "img_values": centred(keys[4], (IMG, KVH * HD), 1.0, 6.0, ((0, 16),)),
        "key_weight": centred(keys[5], (DM, KVH * HD), DM ** -0.5, 0.0625, ((0, 16),)),
        "value_weight": centred(keys[6], (DM, KVH * HD), DM ** -0.5, 0.0625, ((0, 16),)),
        "proj_weight": centred(keys[7], (VW, DM), VW ** -0.5, 0.0625, ((0, 16),)),
        "block_order": jax.random.permutation(keys[8], NB).astype(jnp.int32),
        "owner_counts": uneven_parts(keys[9], OWNERS, NB, CAP, 2).astype(jnp.int32),
    }


CONTRACT_LAST = (((1,), (1,)), ((), ()))
CONTRACT_FIRST = (((0,), (0,)), ((), ()))


def owner_table(block_order, owner_counts, capacity):
    counts = owner_counts.astype(jnp.int32)
    offsets = jnp.cumsum(counts) - counts
    columns = jnp.arange(capacity, dtype=jnp.int32)
    position = offsets[:, None] + columns[None, :]
    living = columns[None, :] < counts[:, None]
    blocks = jnp.arange(block_order.shape[0], dtype=jnp.int32)
    matches = position[:, :, None] == blocks[None, None, :]
    chosen = jnp.sum(jnp.where(matches, block_order[None, None, :], 0), axis=2).astype(jnp.int32)
    return jnp.where(living, chosen, 0).astype(jnp.int32), living


def head_backward(query_head, key_head, value_head, grad_head, output_head, scaling):
    scores = lax.dot_general(query_head, key_head, CONTRACT_LAST, preferred_element_type=jnp.float32) * scaling
    weights = jnp.exp(scores - jax.nn.logsumexp(scores, axis=1, keepdims=True))
    weights_low = weights.astype(jnp.bfloat16)
    dweights = lax.dot_general(grad_head, value_head, CONTRACT_LAST, preferred_element_type=jnp.float32)
    delta = jnp.sum(grad_head.astype(jnp.float32) * output_head.astype(jnp.float32), axis=1, keepdims=True)
    dscores = (weights * (dweights - delta)).astype(jnp.bfloat16)
    grad_query = jnp.dot(dscores, key_head, preferred_element_type=jnp.float32) * scaling
    grad_key = lax.dot_general(dscores, query_head, CONTRACT_FIRST, preferred_element_type=jnp.float32) * scaling
    grad_value = lax.dot_general(weights_low, grad_head, CONTRACT_FIRST, preferred_element_type=jnp.float32)
    return grad_query, jnp.concatenate([grad_key, grad_value], axis=1)


def reference(queries, out_grad, attn_out, img_keys, img_values, key_weight, value_weight, proj_weight, block_order, owner_counts):
    scaling = HD ** -0.5
    group_size = QH // KVH

    def one_head(head_number):
        group_index = (head_number // group_size).astype(jnp.int32)
        column = (head_number * HD).astype(jnp.int32)
        kv_column = (group_index * HD).astype(jnp.int32)
        query_head = lax.dynamic_slice_in_dim(queries, column, HD, 1)
        grad_head = lax.dynamic_slice_in_dim(out_grad, column, HD, 1)
        output_head = lax.dynamic_slice_in_dim(attn_out, column, HD, 1)
        key_head = lax.dynamic_slice_in_dim(img_keys, kv_column, HD, 1)
        value_head = lax.dynamic_slice_in_dim(img_values, kv_column, HD, 1)
        return head_backward(query_head, key_head, value_head, grad_head, output_head, scaling)

    query_grads, pair_grads = lax.map(one_head, jnp.arange(QH, dtype=jnp.int32))
    d_query = jnp.transpose(query_grads, (1, 0, 2)).reshape(TEXT, QH * HD).astype(jnp.bfloat16)
    summed = jnp.sum(pair_grads.reshape(KVH, group_size, IMG, 2, HD), axis=1)
    key_grad = jnp.transpose(summed[:, :, 0], (1, 0, 2)).reshape(IMG, KVH * HD).astype(jnp.bfloat16)
    value_grad = jnp.transpose(summed[:, :, 1], (1, 0, 2)).reshape(IMG, KVH * HD).astype(jnp.bfloat16)
    image_grad = lax.dot_general(key_grad, key_weight, CONTRACT_LAST, preferred_element_type=jnp.float32)
    image_grad = image_grad + lax.dot_general(value_grad, value_weight, CONTRACT_LAST, preferred_element_type=jnp.float32)
    image_grad = image_grad.astype(jnp.bfloat16)
    vision_grad = lax.dot_general(image_grad, proj_weight, CONTRACT_LAST, preferred_element_type=jnp.float32).astype(jnp.bfloat16)
    slots, living = owner_table(block_order, owner_counts, CAP)
    vision_blocks = vision_grad.reshape(NB, BR, VW)
    picked = jnp.take(vision_blocks, slots.reshape(OWNERS * CAP), axis=0).reshape(OWNERS, CAP, BR, VW)
    picked = jnp.where(living[:, :, None, None], picked, jnp.zeros_like(picked))
    d_vision = picked.reshape(OWNERS * CAP * BR, VW)
    return d_query, d_vision
```

```python
import functools

import jax
import jax.numpy as jnp
from jax import lax
from jax.experimental import pallas as pl
from jax.experimental.pallas import tpu as pltpu
from jax.sharding import Mesh
from jax.sharding import PartitionSpec as P

HD = 128
BR = 64
CAP = 4
SCALE = HD**-0.5
LOG2E = 1.4426950408889634

CHIPS = ("zl", "y")
HEADS = ("zh", "xh", "xl")
CTX = ("zl", "y", "co")

LAST = (((1,), (1,)), ((), ()))


def attention_kernel(order, counts, core, kv, q, do, ao, dq, mine, other, gk, gv, kt):
    step = pl.program_id(0)
    keys = kv[:, 0:HD]
    values = kv[:, HD : 2 * HD]

    @pl.when(step == 0)
    def _():
        gk[...] = jnp.zeros_like(gk)
        gv[...] = jnp.zeros_like(gv)
        kt[...] = keys.T

    s = lax.dot_general(keys, q[...], LAST, preferred_element_type=jnp.float32)
    s = s * (SCALE * LOG2E)
    e = jnp.exp2(s - jnp.max(s, axis=0, keepdims=True))
    p = e * (1.0 / jnp.sum(e, axis=0, keepdims=True))
    p_low = p.astype(jnp.bfloat16)
    dp = lax.dot_general(values, do[...], LAST, preferred_element_type=jnp.float32)
    both = do[...].astype(jnp.float32) * ao[...].astype(jnp.float32)
    delta = jnp.sum(both.T, axis=0, keepdims=True)
    ds = (p * (dp - delta)).astype(jnp.bfloat16)
    dq_t = jnp.dot(kt[...], ds, preferred_element_type=jnp.float32) * SCALE
    dq[...] = dq_t.T.astype(jnp.bfloat16)
    gk[...] += jnp.dot(ds, q[...], preferred_element_type=jnp.float32)
    gv[...] += jnp.dot(p_low, do[...], preferred_element_type=jnp.float32)

    @pl.when(step == pl.num_programs(0) - 1)
    def _():
        me = core[0]
        start = jnp.int32(0)
        for chip in range(8):
            begin = [None, None]
            count = [None, None]
            for c in range(2):
                begin[c] = start
                count[c] = counts[2 * chip + c]
                start = start + count[c]
            for out, flip in ((mine, False), (other, True)):
                second = (me == 0) if flip else (me == 1)
                first = jnp.where(second, begin[1], begin[0])
                alive = jnp.where(second, count[1], count[0])
                for slot in range(CAP):
                    block = order[jnp.minimum(first + slot, 31)]
                    owner = block // 2
                    row = (owner % 2) * 1024 + (owner // 2) * 128 + (block % 2) * BR
                    rows = pl.ds(pl.multiple_of(row, BR), BR)
                    keep = jnp.where(slot < alive, 1.0, 0.0).astype(jnp.float32)
                    to = pl.ds(slot * BR, BR)
                    out[chip, 0, to, :] = (gk[rows, :] * (keep * SCALE)).astype(jnp.bfloat16)
                    out[chip, 1, to, :] = (gv[rows, :] * keep).astype(jnp.bfloat16)


def attention(order, counts, core, kv, queries, out_grad, attn_out):
    rows, width = queries.shape
    heads = width // HD
    image = kv.shape[0]
    column = pl.BlockSpec((rows, HD), lambda i: (0, i))
    smem = pl.BlockSpec(memory_space=pltpu.SMEM)
    routed = pl.BlockSpec((8, 2, CAP * BR, HD), lambda i: (0, 0, 0, 0))
    grads = jax.ShapeDtypeStruct((8, 2, CAP * BR, HD), jnp.bfloat16)
    return pl.pallas_call(
        attention_kernel,
        grid=(heads,),
        in_specs=[smem, smem, smem, pl.BlockSpec(kv.shape, lambda i: (0, 0)), column, column, column],
        out_specs=[column, routed, routed],
        out_shape=[jax.ShapeDtypeStruct(queries.shape, jnp.bfloat16), grads, grads],
        scratch_shapes=[
            pltpu.VMEM((image, HD), jnp.float32),
            pltpu.VMEM((image, HD), jnp.float32),
            pltpu.VMEM((HD, image), jnp.bfloat16),
        ],
        compiler_params=pltpu.CompilerParams(vmem_limit_bytes=40 << 20),
        cost_estimate=pl.CostEstimate(
            flops=10 * rows * width * image, transcendentals=rows * heads * image, bytes_accessed=5 << 20
        ),
        name="attention",
    )(order, counts, core, kv, queries, out_grad, attn_out)


def product_kernel(w, wp, out, acc):
    step = pl.program_id(0)

    @pl.when(step == 0)
    def _():
        acc[...] = jnp.zeros_like(acc)

    acc[...] += jnp.dot(wp[...], w[0, 0], preferred_element_type=jnp.float32)

    @pl.when(step == pl.num_programs(0) - 1)
    def _():
        out[...] = acc[...].astype(jnp.bfloat16)


def weight_product(gathered, proj_weight):
    width, model = proj_weight.shape
    xs, zhs, part, cols = gathered.shape
    return pl.pallas_call(
        product_kernel,
        grid=(xs * zhs,),
        in_specs=[
            pl.BlockSpec((1, 1, part, cols), lambda i: (i % 4, i // 4, 0, 0)),
            pl.BlockSpec((width, part), lambda i: (0, i)),
        ],
        out_specs=pl.BlockSpec((width, cols), lambda i: (0, 0)),
        out_shape=jax.ShapeDtypeStruct((width, cols), jnp.bfloat16),
        scratch_shapes=[pltpu.VMEM((width, cols), jnp.float32)],
        compiler_params=pltpu.CompilerParams(vmem_limit_bytes=16 << 20),
        cost_estimate=pl.CostEstimate(
            flops=2 * width * model * cols, transcendentals=0, bytes_accessed=10 << 20
        ),
        name="weight_product",
    )(gathered, proj_weight)


def final_kernel(grads, product, out):
    total = None
    for group in range(16):
        term = lax.dot_general(
            grads[group], product[group % 2, group // 2], LAST, preferred_element_type=jnp.float32
        )
        total = term if total is None else total + term
    out[...] = total.astype(jnp.bfloat16)


def final_product(grads, product):
    rows = grads.shape[1]
    width = product.shape[2]
    return pl.pallas_call(
        final_kernel,
        out_shape=jax.ShapeDtypeStruct((rows, width), jnp.bfloat16),
        in_specs=[pl.BlockSpec(memory_space=pltpu.VMEM)] * 2,
        out_specs=pl.BlockSpec(memory_space=pltpu.VMEM),
        compiler_params=pltpu.CompilerParams(vmem_limit_bytes=16 << 20),
        cost_estimate=pl.CostEstimate(
            flops=2 * rows * width * 2048, transcendentals=0, bytes_accessed=4 << 20
        ),
        name="final_product",
    )(grads, product)


def everywhere(array, axes, count):
    copies = jnp.broadcast_to(array, (count, *array.shape))
    return lax.all_to_all(copies, axes, split_axis=0, concat_axis=0, tiled=True)


def shards(
    queries,
    out_grad,
    attn_out,
    img_keys,
    img_values,
    key_weight,
    value_weight,
    proj_weight,
    block_order,
    owner_counts,
):
    core = lax.axis_index("co")
    chip = lax.axis_index(CHIPS)
    group = lax.axis_index(("zh", "xh"))

    own = jnp.concatenate(
        [
            lax.dynamic_slice_in_dim(img_keys, group * HD, HD, 1),
            lax.dynamic_slice_in_dim(img_values, group * HD, HD, 1),
        ],
        axis=1,
    )
    kv = everywhere(own, CHIPS, 8).reshape(1024, 2 * HD)

    w = jnp.where(
        core == 0,
        lax.dynamic_slice_in_dim(key_weight, chip * HD, HD, 1),
        lax.dynamic_slice_in_dim(value_weight, chip * HD, HD, 1),
    )
    w = everywhere(w, "zh", 4)
    w = everywhere(w, ("xh", "xl"), 4)

    kv = lax.all_gather(kv, "co", axis=0, tiled=True)
    d_query, mine, other = attention(
        block_order, owner_counts, core.reshape(1), kv, queries, out_grad, attn_out
    )
    theirs = lax.ppermute(other, "co", [(0, 1), (1, 0)])
    pair = (mine.astype(jnp.float32) + theirs.astype(jnp.float32)).astype(jnp.bfloat16)
    pieces = lax.all_to_all(
        pair.reshape(16, CAP * BR, HD), ("zl", "y", "xl"), split_axis=0, concat_axis=0, tiled=True
    )
    summed = jnp.sum(pieces.astype(jnp.float32), axis=0).astype(jnp.bfloat16)
    grads = everywhere(summed, HEADS, 16)

    product = weight_product(w, proj_weight)
    product = everywhere(product, CHIPS, 8)
    product = lax.all_gather(product, "co", axis=0, tiled=False)
    d_vision = final_product(grads, product)
    return (d_query, d_vision)


def solution(mesh):
    fine = Mesh(mesh.devices.reshape(2, 4, 2, 4, 2, 2), (*CTX, *HEADS))
    placed = (
        P(CTX, HEADS),
        P(CTX, HEADS),
        P(CTX, HEADS),
        P(CTX, None),
        P(CTX, None),
        P(HEADS, None),
        P(HEADS, None),
        P(HEADS, None),
        P(),
        P(),
    )
    return jax.shard_map(
        shards,
        mesh=fine,
        in_specs=placed,
        out_specs=(P(CTX, HEADS), P(CTX, HEADS)),
        check_vma=False,
    )
```

```python
import functools

import jax
import jax.numpy as jnp
from jax import lax
from jax.experimental import pallas as pl
from jax.experimental.pallas import tpu as pltpu
from jax.sharding import Mesh
from jax.sharding import PartitionSpec as P

HD = 128
BR = 64
CAP = 4
SCALE = HD**-0.5
CHUNK = 512
LOG2E = 1.4426950408889634

CHIPS = ("zl", "y")
HEADS = ("zh", "xh", "xl")
CTX = ("zl", "y", "co")

LAST = (((1,), (1,)), ((), ()))


def route(order, counts, core, gk, gv, mine, other):
    me = core[0]
    start = jnp.int32(0)
    for chip in range(8):
        begin, count = [], []
        for c in range(2):
            begin.append(start)
            count.append(counts[2 * chip + c])
            start = start + count[c]
        for out, second in ((mine, me == 1), (other, me == 0)):
            first = jnp.where(second, begin[1], begin[0])
            alive = jnp.where(second, count[1], count[0])
            for slot in range(CAP):
                block = order[jnp.minimum(first + slot, 31)]
                ctx = block // 2
                away = jnp.where(ctx % 2 == me, 0, 1024)
                row = away + (ctx // 2) * 128 + (block % 2) * BR
                rows = pl.ds(pl.multiple_of(row, BR), BR)
                keep = jnp.where(slot < alive, 1.0, 0.0).astype(jnp.float32)
                to = pl.ds(slot * BR, BR)
                out[chip, 0, to, :] = (gk[rows, :] * (keep * SCALE)).astype(jnp.bfloat16)
                out[chip, 1, to, :] = (gv[rows, :] * keep).astype(jnp.bfloat16)


def attention_kernel(order, counts, core, kv0, kv1, q_ref, do_ref, ao_ref, dq, mine, other, gk, gv, kt):
    half = kv0.shape[0]
    pieces = [(r, at) for r in (kv0, kv1) for at in range(0, half, CHUNK)]
    spans = [slice(i * CHUNK, (i + 1) * CHUNK) for i in range(len(pieces))]
    keys = lambda i: pieces[i][0][pieces[i][1] : pieces[i][1] + CHUNK, 0:HD]
    values = lambda i: pieces[i][0][pieces[i][1] : pieces[i][1] + CHUNK, HD : 2 * HD]
    every = range(len(pieces))
    for i in every:
        kt[:, spans[i]] = keys(i).T
    for head in range(q_ref.shape[1] // HD):
        cols = slice(head * HD, (head + 1) * HD)
        q, do = q_ref[:, cols], do_ref[:, cols]
        s = [lax.dot_general(keys(i), q, LAST, preferred_element_type=jnp.float32) for i in every]
        top = functools.reduce(jnp.maximum, [x.max(axis=0, keepdims=True) for x in s])
        top = top * (SCALE * LOG2E)
        e = [jnp.exp2(x * (SCALE * LOG2E) - top) for x in s]
        inverse = 1.0 / functools.reduce(jnp.add, [x.sum(axis=0, keepdims=True) for x in e])
        both = do.astype(jnp.float32) * ao_ref[:, cols].astype(jnp.float32)
        delta = jnp.sum(both.T, axis=0, keepdims=True)
        dq_t = None
        for i in every:
            dp = lax.dot_general(values(i), do, LAST, preferred_element_type=jnp.float32)
            p = e[i] * inverse
            ds = (p * (dp - delta)).astype(jnp.bfloat16)
            part = jnp.dot(kt[:, spans[i]], ds, preferred_element_type=jnp.float32)
            dq_t = part if dq_t is None else dq_t + part
            key_part = jnp.dot(ds, q, preferred_element_type=jnp.float32)
            value_part = jnp.dot(p.astype(jnp.bfloat16), do, preferred_element_type=jnp.float32)
            if head == 0:
                gk[spans[i]] = key_part
                gv[spans[i]] = value_part
            else:
                gk[spans[i]] += key_part
                gv[spans[i]] += value_part
        dq[:, cols] = (dq_t * SCALE).T.astype(jnp.bfloat16)
    route(order, counts, core, gk, gv, mine, other)


def attention(order, counts, core, kv_here, kv_there, queries, out_grad, attn_out):
    rows, width = queries.shape
    image = 2 * kv_here.shape[0]
    smem = pl.BlockSpec(memory_space=pltpu.SMEM)
    vmem = pl.BlockSpec(memory_space=pltpu.VMEM)
    grads = jax.ShapeDtypeStruct((8, 2, CAP * BR, HD), jnp.bfloat16)
    return pl.pallas_call(
        attention_kernel,
        in_specs=[smem] * 3 + [vmem] * 5,
        out_specs=[vmem] * 3,
        out_shape=[jax.ShapeDtypeStruct(queries.shape, jnp.bfloat16), grads, grads],
        scratch_shapes=[
            pltpu.VMEM((image, HD), jnp.float32),
            pltpu.VMEM((image, HD), jnp.float32),
            pltpu.VMEM((HD, image), jnp.bfloat16),
        ],
        compiler_params=pltpu.CompilerParams(vmem_limit_bytes=24 << 20),
        cost_estimate=pl.CostEstimate(
            flops=10 * rows * width * image, transcendentals=rows * width // HD * image, bytes_accessed=5 << 20
        ),
        name="attention",
    )(order, counts, core, kv_here, kv_there, queries, out_grad, attn_out)


def product_kernel(at, w, wp, out, held, kept, sems, w_sems):
    part = w.shape[1] // 4
    copies, pieces = [], []
    w_copies = [pltpu.make_async_copy(w.at[x], kept.at[x], w_sems.at[x]) for x in range(4)]
    for x in range(4):
        for kz in range(4):
            heads = lax.rem(at[0] + 4 - kz, 4) * 4 + x
            cols = pl.ds(pl.multiple_of(heads * part, part), part)
            i = len(copies)
            copies.append(pltpu.make_async_copy(wp.at[:, cols], held.at[i], sems.at[i]))
            pieces.append((x, kz * part))
    for x in range(4):
        w_copies[x].start()
        for copy in copies[4 * x : 4 * x + 4]:
            copy.start()
    total = None
    for i, (x, row) in enumerate(pieces):
        if row == 0:
            w_copies[x].wait()
        copies[i].wait()
        term = jnp.dot(held[i], kept[x, row : row + part, :], preferred_element_type=jnp.float32)
        total = term if total is None else total + term
    out[...] = total.astype(jnp.bfloat16)


def weight_product(at, w, proj_weight):
    width, model = proj_weight.shape
    vmem = pl.BlockSpec(memory_space=pltpu.VMEM)
    return pl.pallas_call(
        product_kernel,
        in_specs=[pl.BlockSpec(memory_space=pltpu.SMEM)] + [pl.BlockSpec(memory_space=pl.ANY)] * 2,
        out_specs=vmem,
        out_shape=jax.ShapeDtypeStruct((width, HD), jnp.bfloat16),
        scratch_shapes=[
            pltpu.VMEM((16, width, model // 16), jnp.bfloat16),
            pltpu.VMEM(w.shape, jnp.bfloat16),
            pltpu.SemaphoreType.DMA((16,)),
            pltpu.SemaphoreType.DMA((4,)),
        ],
        compiler_params=pltpu.CompilerParams(vmem_limit_bytes=60 << 20),
        cost_estimate=pl.CostEstimate(
            flops=2 * width * model * HD, transcendentals=0, bytes_accessed=10 << 20
        ),
        name="weight_product",
    )(at, w, proj_weight)


def final_kernel(at, grads, *refs):
    here, there, out = refs[:4], refs[4:8], refs[8]
    total = None
    for back in range(4):
        for lane in range(2):
            chip = (at[0] ^ lane) * 4 + lax.rem(at[1] + 4 - back, 4)
            for product, c in ((here[back], at[2]), (there[back], 1 - at[2])):
                term = lax.dot_general(
                    product[lane], grads[2 * chip + c], LAST, preferred_element_type=jnp.float32
                )
                total = term if total is None else total + term
    out[...] = total.astype(jnp.bfloat16)


def final_product(at, grads, here, there):
    rows = grads.shape[1]
    width = here[0].shape[1]
    smem = pl.BlockSpec(memory_space=pltpu.SMEM)
    vmem = pl.BlockSpec(memory_space=pltpu.VMEM)
    return pl.pallas_call(
        final_kernel,
        out_shape=jax.ShapeDtypeStruct((width, rows), jnp.bfloat16),
        in_specs=[smem] + [vmem] * 9,
        out_specs=vmem,
        compiler_params=pltpu.CompilerParams(vmem_limit_bytes=16 << 20),
        cost_estimate=pl.CostEstimate(
            flops=2 * rows * width * 2048, transcendentals=0, bytes_accessed=4 << 20
        ),
        name="final_product",
    )(at, grads, *here, *there)


def everywhere(array, axes, count):
    copies = jnp.broadcast_to(array, (count, *array.shape))
    return lax.all_to_all(copies, axes, split_axis=0, concat_axis=0, tiled=True)


def swap(axis, array):
    return lax.ppermute(array, axis, [(0, 1), (1, 0)])


def ring(array, axes):
    return [array] + [lax.ppermute(array, axes, [(i, (i + k) % 4) for i in range(4)]) for k in (1, 2, 3)]


def shards(
    queries,
    out_grad,
    attn_out,
    img_keys,
    img_values,
    key_weight,
    value_weight,
    proj_weight,
    block_order,
    owner_counts,
):
    core = lax.axis_index("co")
    chip = lax.axis_index(CHIPS)
    group = lax.axis_index(("zh", "xh"))

    w = jnp.where(
        core == 0,
        lax.dynamic_slice_in_dim(key_weight, chip * HD, HD, 1),
        lax.dynamic_slice_in_dim(value_weight, chip * HD, HD, 1),
    )
    w = jnp.concatenate(ring(w, "zh"), axis=0)

    own = jnp.concatenate(
        [
            lax.dynamic_slice_in_dim(img_keys, group * HD, HD, 1),
            lax.dynamic_slice_in_dim(img_values, group * HD, HD, 1),
        ],
        axis=1,
    )
    kv = everywhere(own, CHIPS, 8).reshape(1024, 2 * HD)
    kv, w = lax.optimization_barrier((kv, w))
    w = lax.all_gather(w, ("xh", "xl"), axis=0, tiled=False)
    d_query, mine, other = attention(
        block_order, owner_counts, core.reshape(1), kv, swap("co", kv), queries, out_grad, attn_out
    )
    pair = mine.astype(jnp.float32) + swap("co", other).astype(jnp.float32)
    pieces = lax.all_to_all(
        pair.astype(jnp.bfloat16).reshape(16, CAP * BR, HD),
        ("zl", "y", "xl"),
        split_axis=0,
        concat_axis=0,
        tiled=True,
    )
    summed = jnp.sum(pieces.astype(jnp.float32), axis=0).astype(jnp.bfloat16)
    grads = everywhere(summed, HEADS, 16)

    at = jnp.stack([lax.axis_index(a) for a in CTX])
    product = weight_product(lax.axis_index("zh").reshape(1), w, proj_weight)
    product = jnp.stack([product, swap("zl", product)])
    product = ring(product, "y")
    d_vision = final_product(at, grads, product, [swap("co", p) for p in product])
    return (d_query, d_vision.T)


def solution(mesh):
    fine = Mesh(mesh.devices.reshape(2, 4, 2, 4, 2, 2), (*CTX, *HEADS))
    placed = (
        P(CTX, HEADS),
        P(CTX, HEADS),
        P(CTX, HEADS),
        P(CTX, None),
        P(CTX, None),
        P(HEADS, None),
        P(HEADS, None),
        P(HEADS, None),
        P(),
        P(),
    )
    return jax.shard_map(
        shards,
        mesh=fine,
        in_specs=placed,
        out_specs=(P(CTX, HEADS), P(CTX, HEADS)),
        check_vma=False,
    )
```

```python
import functools

import jax
import jax.numpy as jnp
from jax import lax
from jax.experimental import pallas as pl
from jax.experimental.pallas import tpu as pltpu
from jax.sharding import Mesh
from jax.sharding import PartitionSpec as P

HD = 128
BR = 64
CAP = 4
SCALE = HD**-0.5
CHUNK = 512
LOG2E = 1.4426950408889634

CHIPS = ("zl", "y")
HEADS = ("zh", "xh", "xl")
CTX = ("zl", "y", "co")

LAST = (((1,), (1,)), ((), ()))


def route(order, counts, core, gk, gv, mine, other):
    me = core[0]
    start = jnp.int32(0)
    for chip in range(8):
        begin, count = [], []
        for c in range(2):
            begin.append(start)
            count.append(counts[2 * chip + c])
            start = start + count[c]
        for out, second in ((mine, me == 1), (other, me == 0)):
            first = jnp.where(second, begin[1], begin[0])
            alive = jnp.where(second, count[1], count[0])
            for slot in range(CAP):
                block = order[jnp.minimum(first + slot, 31)]
                ctx = block // 2
                away = jnp.where(ctx % 2 == me, 0, 1024)
                row = away + (ctx // 2) * 128 + (block % 2) * BR
                rows = pl.ds(pl.multiple_of(row, BR), BR)
                keep = jnp.where(slot < alive, 1.0, 0.0).astype(jnp.float32)
                to = pl.ds(slot * BR, BR)
                out[chip, 0, to, :] = (gk[rows, :] * (keep * SCALE)).astype(jnp.bfloat16)
                out[chip, 1, to, :] = (gv[rows, :] * keep).astype(jnp.bfloat16)


def attention_kernel(order, counts, core, kv0, kv1, q_ref, do_ref, ao_ref, dq, mine, other, gk, gv, kt):
    half = kv0.shape[0]
    pieces = [(r, at) for r in (kv0, kv1) for at in range(0, half, CHUNK)]
    spans = [slice(i * CHUNK, (i + 1) * CHUNK) for i in range(len(pieces))]
    keys = lambda i: pieces[i][0][pieces[i][1] : pieces[i][1] + CHUNK, 0:HD]
    values = lambda i: pieces[i][0][pieces[i][1] : pieces[i][1] + CHUNK, HD : 2 * HD]
    every = range(len(pieces))
    for i in every:
        kt[:, spans[i]] = keys(i).T
    for head in range(q_ref.shape[1] // HD):
        cols = slice(head * HD, (head + 1) * HD)
        q, do = q_ref[:, cols], do_ref[:, cols]
        s = [lax.dot_general(keys(i), q, LAST, preferred_element_type=jnp.float32) for i in every]
        top = functools.reduce(jnp.maximum, [x.max(axis=0, keepdims=True) for x in s])
        top = top * (SCALE * LOG2E)
        e = [jnp.exp2(x * (SCALE * LOG2E) - top) for x in s]
        inverse = 1.0 / functools.reduce(jnp.add, [x.sum(axis=0, keepdims=True) for x in e])
        both = do.astype(jnp.float32) * ao_ref[:, cols].astype(jnp.float32)
        delta = jnp.sum(both.T, axis=0, keepdims=True)
        dq_t = None
        for i in every:
            dp = lax.dot_general(values(i), do, LAST, preferred_element_type=jnp.float32)
            p = e[i] * inverse
            ds = (p * (dp - delta)).astype(jnp.bfloat16)
            part = jnp.dot(kt[:, spans[i]], ds, preferred_element_type=jnp.float32)
            dq_t = part if dq_t is None else dq_t + part
            key_part = jnp.dot(ds, q, preferred_element_type=jnp.float32)
            value_part = jnp.dot(p.astype(jnp.bfloat16), do, preferred_element_type=jnp.float32)
            if head == 0:
                gk[spans[i]] = key_part
                gv[spans[i]] = value_part
            else:
                gk[spans[i]] += key_part
                gv[spans[i]] += value_part
        dq[:, cols] = (dq_t * SCALE).T.astype(jnp.bfloat16)
    route(order, counts, core, gk, gv, mine, other)


def attention(order, counts, core, kv_here, kv_there, queries, out_grad, attn_out):
    rows, width = queries.shape
    image = 2 * kv_here.shape[0]
    smem = pl.BlockSpec(memory_space=pltpu.SMEM)
    vmem = pl.BlockSpec(memory_space=pltpu.VMEM)
    grads = jax.ShapeDtypeStruct((8, 2, CAP * BR, HD), jnp.bfloat16)
    return pl.pallas_call(
        attention_kernel,
        in_specs=[smem] * 3 + [vmem] * 5,
        out_specs=[vmem] * 3,
        out_shape=[jax.ShapeDtypeStruct(queries.shape, jnp.bfloat16), grads, grads],
        scratch_shapes=[
            pltpu.VMEM((image, HD), jnp.float32),
            pltpu.VMEM((image, HD), jnp.float32),
            pltpu.VMEM((HD, image), jnp.bfloat16),
        ],
        compiler_params=pltpu.CompilerParams(vmem_limit_bytes=24 << 20),
        cost_estimate=pl.CostEstimate(
            flops=10 * rows * width * image, transcendentals=rows * width // HD * image, bytes_accessed=5 << 20
        ),
        name="attention",
    )(order, counts, core, kv_here, kv_there, queries, out_grad, attn_out)


def product_kernel(at, w0, w1, w2, w3, wp, out):
    part = w0.shape[0] // 4
    total = None
    for kx, w in enumerate((w0, w1, w2, w3)):
        for kz in range(4):
            heads = lax.rem(at[0] + 4 - kz, 4) * 4 + lax.rem(at[1] + 4 - kx, 4)
            cols = pl.ds(pl.multiple_of(heads * part, part), part)
            term = jnp.dot(wp[:, cols], w[kz * part : (kz + 1) * part, :], preferred_element_type=jnp.float32)
            total = term if total is None else total + term
    out[...] = total.astype(jnp.bfloat16)


def weight_product(at, pieces, proj_weight):
    width, model = proj_weight.shape
    vmem = pl.BlockSpec(memory_space=pltpu.VMEM)
    return pl.pallas_call(
        product_kernel,
        in_specs=[pl.BlockSpec(memory_space=pltpu.SMEM)] + [vmem] * 5,
        out_specs=vmem,
        out_shape=jax.ShapeDtypeStruct((width, HD), jnp.bfloat16),
        compiler_params=pltpu.CompilerParams(vmem_limit_bytes=14 << 20),
        cost_estimate=pl.CostEstimate(
            flops=2 * width * model * HD, transcendentals=0, bytes_accessed=10 << 20
        ),
        name="weight_product",
    )(at, *pieces, proj_weight)


def final_kernel(at, grads, *refs):
    here, there, out = refs[:4], refs[4:8], refs[8]
    total = None
    for back in range(4):
        for lane in range(2):
            chip = (at[0] ^ lane) * 4 + lax.rem(at[1] + 4 - back, 4)
            for product, c in ((here[back], at[2]), (there[back], 1 - at[2])):
                term = lax.dot_general(
                    product[lane], grads[2 * chip + c], LAST, preferred_element_type=jnp.float32
                )
                total = term if total is None else total + term
    out[...] = total.astype(jnp.bfloat16)


def final_product(at, grads, here, there):
    rows = grads.shape[1]
    width = here[0].shape[1]
    smem = pl.BlockSpec(memory_space=pltpu.SMEM)
    vmem = pl.BlockSpec(memory_space=pltpu.VMEM)
    return pl.pallas_call(
        final_kernel,
        out_shape=jax.ShapeDtypeStruct((width, rows), jnp.bfloat16),
        in_specs=[smem] + [vmem] * 9,
        out_specs=vmem,
        compiler_params=pltpu.CompilerParams(vmem_limit_bytes=16 << 20),
        cost_estimate=pl.CostEstimate(
            flops=2 * rows * width * 2048, transcendentals=0, bytes_accessed=4 << 20
        ),
        name="final_product",
    )(at, grads, *here, *there)


def everywhere(array, axes, count):
    copies = jnp.broadcast_to(array, (count, *array.shape))
    return lax.all_to_all(copies, axes, split_axis=0, concat_axis=0, tiled=True)


def swap(axis, array):
    return lax.ppermute(array, axis, [(0, 1), (1, 0)])


def ring(array, axes):
    return [array] + [lax.ppermute(array, axes, [(i, (i + k) % 4) for i in range(4)]) for k in (1, 2, 3)]


def shards(
    queries,
    out_grad,
    attn_out,
    img_keys,
    img_values,
    key_weight,
    value_weight,
    proj_weight,
    block_order,
    owner_counts,
):
    core = lax.axis_index("co")
    chip = lax.axis_index(CHIPS)
    group = lax.axis_index(("zh", "xh"))

    w = jnp.where(
        core == 0,
        lax.dynamic_slice_in_dim(key_weight, chip * HD, HD, 1),
        lax.dynamic_slice_in_dim(value_weight, chip * HD, HD, 1),
    )
    w = jnp.concatenate(ring(w, "zh"), axis=0)

    own = jnp.concatenate(
        [
            lax.dynamic_slice_in_dim(img_keys, group * HD, HD, 1),
            lax.dynamic_slice_in_dim(img_values, group * HD, HD, 1),
        ],
        axis=1,
    )
    kv = everywhere(own, CHIPS, 8).reshape(1024, 2 * HD)
    kv, w = lax.optimization_barrier((kv, w))
    w = ring(w, ("xh", "xl"))
    d_query, mine, other = attention(
        block_order, owner_counts, core.reshape(1), kv, swap("co", kv), queries, out_grad, attn_out
    )
    other, *w = lax.optimization_barrier((other, *w))
    pair = mine.astype(jnp.float32) + swap("co", other).astype(jnp.float32)
    pair = pair.astype(jnp.bfloat16).reshape(16, CAP * BR, HD)
    pieces = lax.all_to_all(
        pair,
        ("zl", "y", "xl"),
        split_axis=0,
        concat_axis=0,
        tiled=True,
    )
    summed = jnp.sum(pieces.astype(jnp.float32), axis=0).astype(jnp.bfloat16)

    at = jnp.stack([lax.axis_index(a) for a in CTX])
    heads_at = jnp.stack([lax.axis_index("zh"), lax.axis_index(("xh", "xl"))])
    product = weight_product(heads_at, w, proj_weight)
    product = jnp.stack([product, swap("zl", product)])
    summed, product = lax.optimization_barrier((summed, product))
    grads = everywhere(summed, HEADS, 16)
    product = ring(product, "y")
    d_vision = final_product(at, grads, product, [swap("co", p) for p in product])
    return (d_query, d_vision.T)


def solution(mesh):
    fine = Mesh(mesh.devices.reshape(2, 4, 2, 4, 2, 2), (*CTX, *HEADS))
    placed = (
        P(CTX, HEADS),
        P(CTX, HEADS),
        P(CTX, HEADS),
        P(CTX, None),
        P(CTX, None),
        P(HEADS, None),
        P(HEADS, None),
        P(HEADS, None),
        P(),
        P(),
    )
    return jax.shard_map(
        shards,
        mesh=fine,
        in_specs=placed,
        out_specs=(P(CTX, HEADS), P(CTX, HEADS)),
        check_vma=False,
    )
```

```python
import functools

import jax
import jax.numpy as jnp
from jax import lax
from jax.experimental import pallas as pl
from jax.experimental.pallas import tpu as pltpu
from jax.sharding import Mesh
from jax.sharding import PartitionSpec as P

HD = 128
BR = 64
CAP = 4
SCALE = HD**-0.5
CHUNK = 512
LOG2E = 1.4426950408889634

CHIPS = ("zl", "y")
HEADS = ("zh", "xh", "xl")
CTX = ("zl", "y", "co")

LAST = (((1,), (1,)), ((), ()))


def route(order, counts, core, gk, gv, mine, other):
    me = core[0]
    start = jnp.int32(0)
    for chip in range(8):
        begin, count = [], []
        for c in range(2):
            begin.append(start)
            count.append(counts[2 * chip + c])
            start = start + count[c]
        for out, second in ((mine, me == 1), (other, me == 0)):
            first = jnp.where(second, begin[1], begin[0])
            alive = jnp.where(second, count[1], count[0])
            for slot in range(CAP):
                block = order[jnp.minimum(first + slot, 31)]
                ctx = block // 2
                away = jnp.where(ctx % 2 == me, 0, 1024)
                row = away + (ctx // 2) * 128 + (block % 2) * BR
                rows = pl.ds(pl.multiple_of(row, BR), BR)
                keep = jnp.where(slot < alive, 1.0, 0.0).astype(jnp.float32)
                to = pl.ds(slot * BR, BR)
                out[chip, 0, to, :] = (gk[rows, :] * (keep * SCALE)).astype(jnp.bfloat16)
                out[chip, 1, to, :] = (gv[rows, :] * keep).astype(jnp.bfloat16)


def attention_kernel(order, counts, core, kv0, kv1, q_ref, do_ref, ao_ref, dq, mine, other, gk, gv, kt):
    half = kv0.shape[0]
    pieces = [(r, at) for r in (kv0, kv1) for at in range(0, half, CHUNK)]
    spans = [slice(i * CHUNK, (i + 1) * CHUNK) for i in range(len(pieces))]
    keys = lambda i: pieces[i][0][pieces[i][1] : pieces[i][1] + CHUNK, 0:HD]
    values = lambda i: pieces[i][0][pieces[i][1] : pieces[i][1] + CHUNK, HD : 2 * HD]
    every = range(len(pieces))
    for i in every:
        kt[:, spans[i]] = keys(i).T
    for head in range(q_ref.shape[1] // HD):
        cols = slice(head * HD, (head + 1) * HD)
        q, do = q_ref[:, cols], do_ref[:, cols]
        s = [lax.dot_general(keys(i), q, LAST, preferred_element_type=jnp.float32) for i in every]
        top = functools.reduce(jnp.maximum, [x.max(axis=0, keepdims=True) for x in s])
        top = top * (SCALE * LOG2E)
        e = [jnp.exp2(x * (SCALE * LOG2E) - top) for x in s]
        inverse = 1.0 / functools.reduce(jnp.add, [x.sum(axis=0, keepdims=True) for x in e])
        both = do.astype(jnp.float32) * ao_ref[:, cols].astype(jnp.float32)
        delta = jnp.sum(both.T, axis=0, keepdims=True)
        dq_t = None
        for i in every:
            dp = lax.dot_general(values(i), do, LAST, preferred_element_type=jnp.float32)
            p = e[i] * inverse
            ds = (p * (dp - delta)).astype(jnp.bfloat16)
            part = jnp.dot(kt[:, spans[i]], ds, preferred_element_type=jnp.float32)
            dq_t = part if dq_t is None else dq_t + part
            key_part = jnp.dot(ds, q, preferred_element_type=jnp.float32)
            value_part = jnp.dot(p.astype(jnp.bfloat16), do, preferred_element_type=jnp.float32)
            if head == 0:
                gk[spans[i]] = key_part
                gv[spans[i]] = value_part
            else:
                gk[spans[i]] += key_part
                gv[spans[i]] += value_part
        dq[:, cols] = (dq_t * SCALE).T.astype(jnp.bfloat16)
    route(order, counts, core, gk, gv, mine, other)


def attention(order, counts, core, kv_here, kv_there, queries, out_grad, attn_out):
    rows, width = queries.shape
    image = 2 * kv_here.shape[0]
    smem = pl.BlockSpec(memory_space=pltpu.SMEM)
    vmem = pl.BlockSpec(memory_space=pltpu.VMEM)
    grads = jax.ShapeDtypeStruct((8, 2, CAP * BR, HD), jnp.bfloat16)
    return pl.pallas_call(
        attention_kernel,
        in_specs=[smem] * 3 + [vmem] * 5,
        out_specs=[vmem] * 3,
        out_shape=[jax.ShapeDtypeStruct(queries.shape, jnp.bfloat16), grads, grads],
        scratch_shapes=[
            pltpu.VMEM((image, HD), jnp.float32),
            pltpu.VMEM((image, HD), jnp.float32),
            pltpu.VMEM((HD, image), jnp.bfloat16),
        ],
        compiler_params=pltpu.CompilerParams(vmem_limit_bytes=24 << 20),
        cost_estimate=pl.CostEstimate(
            flops=10 * rows * width * image, transcendentals=rows * width // HD * image, bytes_accessed=5 << 20
        ),
        name="attention",
    )(order, counts, core, kv_here, kv_there, queries, out_grad, attn_out)


def product_kernel(at, w0, w1, w2, w3, wp, out):
    part = w0.shape[0] // 4
    total = None
    for kx, w in enumerate((w0, w1, w2, w3)):
        for kz in range(4):
            heads = lax.rem(at[0] + 4 - kz, 4) * 4 + lax.rem(at[1] + 4 - kx, 4)
            cols = pl.ds(pl.multiple_of(heads * part, part), part)
            term = jnp.dot(wp[:, cols], w[kz * part : (kz + 1) * part, :], preferred_element_type=jnp.float32)
            total = term if total is None else total + term
    out[...] = total.astype(jnp.bfloat16)


def weight_product(at, pieces, proj_weight):
    width, model = proj_weight.shape
    vmem = pl.BlockSpec(memory_space=pltpu.VMEM)
    return pl.pallas_call(
        product_kernel,
        in_specs=[pl.BlockSpec(memory_space=pltpu.SMEM)] + [vmem] * 5,
        out_specs=vmem,
        out_shape=jax.ShapeDtypeStruct((width, HD), jnp.bfloat16),
        compiler_params=pltpu.CompilerParams(vmem_limit_bytes=14 << 20),
        cost_estimate=pl.CostEstimate(
            flops=40 * width * model * HD, transcendentals=0, bytes_accessed=10 << 20
        ),
        name="weight_product",
    )(at, *pieces, proj_weight)


def final_kernel(at, grads, *refs):
    here, there, out = refs[:4], refs[4:8], refs[8]
    total = None
    for back in range(4):
        for lane in range(2):
            chip = (at[0] ^ lane) * 4 + lax.rem(at[1] + 4 - back, 4)
            for product, c in ((here[back], at[2]), (there[back], 1 - at[2])):
                term = lax.dot_general(
                    product[lane], grads[2 * chip + c], LAST, preferred_element_type=jnp.float32
                )
                total = term if total is None else total + term
    out[...] = total.astype(jnp.bfloat16)


def final_product(at, grads, here, there):
    rows = grads.shape[1]
    width = here[0].shape[1]
    smem = pl.BlockSpec(memory_space=pltpu.SMEM)
    vmem = pl.BlockSpec(memory_space=pltpu.VMEM)
    return pl.pallas_call(
        final_kernel,
        out_shape=jax.ShapeDtypeStruct((width, rows), jnp.bfloat16),
        in_specs=[smem] + [vmem] * 9,
        out_specs=vmem,
        compiler_params=pltpu.CompilerParams(vmem_limit_bytes=16 << 20),
        cost_estimate=pl.CostEstimate(
            flops=2 * rows * width * 2048, transcendentals=0, bytes_accessed=4 << 20
        ),
        name="final_product",
    )(at, grads, *here, *there)


def everywhere(array, axes, count):
    copies = jnp.broadcast_to(array, (count, *array.shape))
    return lax.all_to_all(copies, axes, split_axis=0, concat_axis=0, tiled=True)


def swap(axis, array):
    return lax.ppermute(array, axis, [(0, 1), (1, 0)])


def ring(array, axes):
    return [array] + [lax.ppermute(array, axes, [(i, (i + k) % 4) for i in range(4)]) for k in (1, 2, 3)]


def shards(
    queries,
    out_grad,
    attn_out,
    img_keys,
    img_values,
    key_weight,
    value_weight,
    proj_weight,
    block_order,
    owner_counts,
):
    core = lax.axis_index("co")
    chip = lax.axis_index(CHIPS)
    group = lax.axis_index(("zh", "xh"))

    w = jnp.where(
        core == 0,
        lax.dynamic_slice_in_dim(key_weight, chip * HD, HD, 1),
        lax.dynamic_slice_in_dim(value_weight, chip * HD, HD, 1),
    )
    w = jnp.concatenate(ring(w, "zh"), axis=0)

    own = jnp.concatenate(
        [
            lax.dynamic_slice_in_dim(img_keys, group * HD, HD, 1),
            lax.dynamic_slice_in_dim(img_values, group * HD, HD, 1),
        ],
        axis=1,
    )
    kv = everywhere(own, CHIPS, 8).reshape(1024, 2 * HD)
    kv, w = lax.optimization_barrier((kv, w))
    w = ring(w, ("xh", "xl"))
    d_query, mine, other = attention(
        block_order, owner_counts, core.reshape(1), kv, swap("co", kv), queries, out_grad, attn_out
    )
    pair = mine.astype(jnp.float32) + swap("co", other).astype(jnp.float32)
    pair = pair.astype(jnp.bfloat16).reshape(16, CAP * BR, HD)
    pieces = lax.all_to_all(
        pair,
        ("zl", "y", "xl"),
        split_axis=0,
        concat_axis=0,
        tiled=True,
    )
    summed = jnp.sum(pieces.astype(jnp.float32), axis=0).astype(jnp.bfloat16)

    at = jnp.stack([lax.axis_index(a) for a in CTX])
    heads_at = jnp.stack([lax.axis_index("zh"), lax.axis_index(("xh", "xl"))])
    product = weight_product(heads_at, w, proj_weight)
    product = jnp.stack([product, swap("zl", product)])
    grads = everywhere(summed, HEADS, 16)
    product = ring(product, "y")
    d_vision = final_product(at, grads, product, [swap("co", p) for p in product])
    return (d_query, d_vision.T)


def solution(mesh):
    fine = Mesh(mesh.devices.reshape(2, 4, 2, 4, 2, 2), (*CTX, *HEADS))
    placed = (
        P(CTX, HEADS),
        P(CTX, HEADS),
        P(CTX, HEADS),
        P(CTX, None),
        P(CTX, None),
        P(HEADS, None),
        P(HEADS, None),
        P(HEADS, None),
        P(),
        P(),
    )
    return jax.shard_map(
        shards,
        mesh=fine,
        in_specs=placed,
        out_specs=(P(CTX, HEADS), P(CTX, HEADS)),
        check_vma=False,
    )
```

```python
import functools

import jax
import jax.numpy as jnp
from jax import lax
from jax.experimental import pallas as pl
from jax.experimental.pallas import tpu as pltpu
from jax.sharding import Mesh
from jax.sharding import PartitionSpec as P

HD = 128
BR = 64
CAP = 4
SCALE = HD**-0.5
CHUNK = 512
LOG2E = 1.4426950408889634

CHIPS = ("zl", "y")
HEADS = ("zh", "xh", "xl")
X = ("xh", "xl")
CTX = ("zl", "y", "co")

LAST = (((1,), (1,)), ((), ()))


def route(order, counts, core, gk, gv, mine, other):
    me = core[0]
    start = jnp.int32(0)
    for chip in range(8):
        begin, count = [], []
        for c in range(2):
            begin.append(start)
            count.append(counts[2 * chip + c])
            start = start + count[c]
        for out, second in ((mine, me == 1), (other, me == 0)):
            first = jnp.where(second, begin[1], begin[0])
            alive = jnp.where(second, count[1], count[0])
            for slot in range(CAP):
                block = order[jnp.minimum(first + slot, 31)]
                ctx = block // 2
                away = jnp.where(ctx % 2 == me, 0, 1024)
                row = away + (ctx // 2) * 128 + (block % 2) * BR
                rows = pl.ds(pl.multiple_of(row, BR), BR)
                keep = jnp.where(slot < alive, 1.0, 0.0).astype(jnp.float32)
                to = pl.ds(slot * BR, BR)
                out[chip, 0, to, :] = (gk[rows, :] * (keep * SCALE)).astype(jnp.bfloat16)
                out[chip, 1, to, :] = (gv[rows, :] * keep).astype(jnp.bfloat16)


def attention_kernel(order, counts, core, kv0, kv1, kv2, q_ref, do_ref, ao_ref, dq, mine, other, gk, gv, kt):
    pieces = [(r, at) for r in (kv0, kv1, kv2) for at in range(0, r.shape[0], CHUNK)]
    spans = [slice(i * CHUNK, (i + 1) * CHUNK) for i in range(len(pieces))]
    keys = lambda i: pieces[i][0][pieces[i][1] : pieces[i][1] + CHUNK, 0:HD]
    values = lambda i: pieces[i][0][pieces[i][1] : pieces[i][1] + CHUNK, HD : 2 * HD]
    every = range(len(pieces))
    for i in every:
        kt[:, spans[i]] = keys(i).T
    for head in range(q_ref.shape[1] // HD):
        cols = slice(head * HD, (head + 1) * HD)
        q, do = q_ref[:, cols], do_ref[:, cols]
        s = [lax.dot_general(keys(i), q, LAST, preferred_element_type=jnp.float32) for i in every]
        top = functools.reduce(jnp.maximum, [x.max(axis=0, keepdims=True) for x in s])
        top = top * (SCALE * LOG2E)
        e = [jnp.exp2(x * (SCALE * LOG2E) - top) for x in s]
        inverse = 1.0 / functools.reduce(jnp.add, [x.sum(axis=0, keepdims=True) for x in e])
        both = do.astype(jnp.float32) * ao_ref[:, cols].astype(jnp.float32)
        delta = jnp.sum(both.T, axis=0, keepdims=True)
        dq_t = None
        for i in every:
            dp = lax.dot_general(values(i), do, LAST, preferred_element_type=jnp.float32)
            p = e[i] * inverse
            ds = (p * (dp - delta)).astype(jnp.bfloat16)
            part = jnp.dot(kt[:, spans[i]], ds, preferred_element_type=jnp.float32)
            dq_t = part if dq_t is None else dq_t + part
            key_part = jnp.dot(ds, q, preferred_element_type=jnp.float32)
            value_part = jnp.dot(p.astype(jnp.bfloat16), do, preferred_element_type=jnp.float32)
            if head == 0:
                gk[spans[i]] = key_part
                gv[spans[i]] = value_part
            else:
                gk[spans[i]] += key_part
                gv[spans[i]] += value_part
        dq[:, cols] = (dq_t * SCALE).T.astype(jnp.bfloat16)
    route(order, counts, core, gk, gv, mine, other)


def attention(order, counts, core, kv_here, kv_there, queries, out_grad, attn_out):
    rows, width = queries.shape
    image = 2 * kv_here.shape[0]
    smem = pl.BlockSpec(memory_space=pltpu.SMEM)
    vmem = pl.BlockSpec(memory_space=pltpu.VMEM)
    grads = jax.ShapeDtypeStruct((8, 2, CAP * BR, HD), jnp.bfloat16)
    return pl.pallas_call(
        attention_kernel,
        in_specs=[smem] * 3 + [vmem] * 6,
        out_specs=[vmem] * 3,
        out_shape=[jax.ShapeDtypeStruct(queries.shape, jnp.bfloat16), grads, grads],
        scratch_shapes=[
            pltpu.VMEM((image, HD), jnp.float32),
            pltpu.VMEM((image, HD), jnp.float32),
            pltpu.VMEM((HD, image), jnp.bfloat16),
        ],
        compiler_params=pltpu.CompilerParams(vmem_limit_bytes=24 << 20),
        cost_estimate=pl.CostEstimate(
            flops=0, transcendentals=0, bytes_accessed=0
        ),
        name="attention",
    )(order, counts, core, kv_here, *kv_there, queries, out_grad, attn_out)


def join_kernel(a, b, c, d, out):
    part = a.shape[0]
    for i, ref in enumerate((a, b, c, d)):
        out[i * part : (i + 1) * part, :] = ref[...]


def join(arrays, flops):
    rows, cols = arrays[0].shape
    vmem = pl.BlockSpec(memory_space=pltpu.VMEM)
    return pl.pallas_call(
        join_kernel,
        in_specs=[vmem] * 4,
        out_specs=vmem,
        out_shape=jax.ShapeDtypeStruct((4 * rows, cols), jnp.bfloat16),
        compiler_params=pltpu.CompilerParams(vmem_limit_bytes=4 << 20),
        cost_estimate=pl.CostEstimate(flops=flops, transcendentals=0, bytes_accessed=1 << 20),
        name="join",
    )(*arrays)


def product_kernel(at, w0, w1, w2, w3, wp, out):
    part = w0.shape[0] // 4
    total = None
    for kx, w in enumerate((w0, w1, w2, w3)):
        for kz in range(4):
            heads = lax.rem(at[0] + 4 - kz, 4) * 4 + lax.rem(at[1] + 4 - kx, 4)
            cols = pl.ds(pl.multiple_of(heads * part, part), part)
            term = jnp.dot(wp[:, cols], w[kz * part : (kz + 1) * part, :], preferred_element_type=jnp.float32)
            total = term if total is None else total + term
    out[...] = total.astype(jnp.bfloat16)


def weight_product(at, pieces, proj_weight):
    width, model = proj_weight.shape
    vmem = pl.BlockSpec(memory_space=pltpu.VMEM)
    return pl.pallas_call(
        product_kernel,
        in_specs=[pl.BlockSpec(memory_space=pltpu.SMEM)] + [vmem] * 5,
        out_specs=vmem,
        out_shape=jax.ShapeDtypeStruct((width, HD), jnp.bfloat16),
        compiler_params=pltpu.CompilerParams(vmem_limit_bytes=14 << 20),
        cost_estimate=pl.CostEstimate(
            flops=2 * width * model * HD, transcendentals=0, bytes_accessed=10 << 20
        ),
        name="weight_product",
    )(at, *pieces, proj_weight)


def final_kernel(at, heads_at, *refs):
    grads, here, there, out, held = refs[:4], refs[4:8], refs[8:12], refs[12], refs[13]
    rows = out.shape[1]
    for kx in range(4):
        for kz in range(4):
            heads = lax.rem(heads_at[0] + 4 - kz, 4) * 4 + lax.rem(heads_at[1] + 4 - kx, 4)
            held[heads] = grads[kx][kz * rows : (kz + 1) * rows, :]
    total = None
    for back in range(4):
        for lane in range(2):
            chip = (at[0] ^ lane) * 4 + lax.rem(at[1] + 4 - back, 4)
            term = lax.dot_general(
                jnp.concatenate([here[back][lane], there[back][lane]], axis=1),
                jnp.concatenate([held[2 * chip + at[2]], held[2 * chip + 1 - at[2]]], axis=1),
                LAST,
                preferred_element_type=jnp.float32,
            )
            total = term if total is None else total + term
    out[...] = total.astype(jnp.bfloat16)


def final_product(at, heads_at, grads, here, there):
    rows = grads[0].shape[0] // 4
    width = here[0].shape[1]
    smem = pl.BlockSpec(memory_space=pltpu.SMEM)
    vmem = pl.BlockSpec(memory_space=pltpu.VMEM)
    return pl.pallas_call(
        final_kernel,
        out_shape=jax.ShapeDtypeStruct((width, rows), jnp.bfloat16),
        in_specs=[smem] * 2 + [vmem] * 12,
        out_specs=vmem,
        scratch_shapes=[pltpu.VMEM((16, rows, HD), jnp.bfloat16)],
        compiler_params=pltpu.CompilerParams(vmem_limit_bytes=16 << 20),
        cost_estimate=pl.CostEstimate(
            flops=2 * rows * width * 2048, transcendentals=0, bytes_accessed=4 << 20
        ),
        name="final_product",
    )(at, heads_at, *grads, *here, *there)


def everywhere(array, axes, count):
    copies = jnp.broadcast_to(array, (count, *array.shape))
    return lax.all_to_all(copies, axes, split_axis=0, concat_axis=0, tiled=True)


def swap(axis, array):
    return lax.ppermute(array, axis, [(0, 1), (1, 0)])


def ring(array, axes):
    return [array] + [lax.ppermute(array, axes, [(i, (i + k) % 4) for i in range(4)]) for k in (1, 2, 3)]


def shards(
    queries,
    out_grad,
    attn_out,
    img_keys,
    img_values,
    key_weight,
    value_weight,
    proj_weight,
    block_order,
    owner_counts,
):
    core = lax.axis_index("co")
    chip = lax.axis_index(CHIPS)
    group = lax.axis_index(("zh", "xh"))

    w = jnp.where(
        core == 0,
        lax.dynamic_slice_in_dim(key_weight, chip * HD, HD, 1),
        lax.dynamic_slice_in_dim(value_weight, chip * HD, HD, 1),
    )
    w = join(ring(w, "zh"), 100 << 30)

    own = jnp.concatenate(
        [
            lax.dynamic_slice_in_dim(img_keys, group * HD, HD, 1),
            lax.dynamic_slice_in_dim(img_values, group * HD, HD, 1),
        ],
        axis=1,
    )
    kv = everywhere(own, CHIPS, 8).reshape(1024, 2 * HD)
    w = ring(w, ("xh", "xl"))
    d_query, mine, other = attention(
        block_order, owner_counts, core.reshape(1), kv, [swap("co", kv[:512]), swap("co", kv[512:])], queries, out_grad, attn_out
    )
    other, *w = lax.optimization_barrier((other, *w))
    pair = mine.astype(jnp.float32) + swap("co", other).astype(jnp.float32)
    pair = pair.astype(jnp.bfloat16).reshape(16, CAP * BR, HD)
    pieces = lax.all_to_all(
        pair,
        ("zl", "y", "xl"),
        split_axis=0,
        concat_axis=0,
        tiled=True,
    )
    summed = jnp.sum(pieces.astype(jnp.float32), axis=0).astype(jnp.bfloat16)

    at = jnp.stack([lax.axis_index(a) for a in CTX])
    heads_at = jnp.stack([lax.axis_index("zh"), lax.axis_index(("xh", "xl"))])
    product = weight_product(heads_at, w, proj_weight)
    product = jnp.stack([product, swap("zl", product)])
    summed, product = lax.optimization_barrier((summed, product))
    grads = ring(join(ring(summed, "zh"), 0), X)
    product = ring(product, "y")
    d_vision = final_product(at, heads_at, grads, product, [swap("co", p) for p in product])
    return (d_query, d_vision.T)


def solution(mesh):
    fine = Mesh(mesh.devices.reshape(2, 4, 2, 4, 2, 2), (*CTX, *HEADS))
    placed = (
        P(CTX, HEADS),
        P(CTX, HEADS),
        P(CTX, HEADS),
        P(CTX, None),
        P(CTX, None),
        P(HEADS, None),
        P(HEADS, None),
        P(HEADS, None),
        P(),
        P(),
    )
    return jax.shard_map(
        shards,
        mesh=fine,
        in_specs=placed,
        out_specs=(P(CTX, HEADS), P(CTX, HEADS)),
        check_vma=False,
    )
```

```python
import functools

import jax
import jax.numpy as jnp
from jax import lax
from jax.experimental import pallas as pl
from jax.experimental.pallas import tpu as pltpu
from jax.sharding import Mesh
from jax.sharding import PartitionSpec as P

HD = 128
BR = 64
CAP = 4
SCALE = HD**-0.5
CHUNK = 512
LOG2E = 1.4426950408889634

CHIPS = ("zl", "y")
HEADS = ("zh", "xh", "xl")
X = ("xh", "xl")
CTX = ("zl", "y", "co")

LAST = (((1,), (1,)), ((), ()))


def route(order, counts, core, gk, gv, mine, other):
    me = core[0]
    start = jnp.int32(0)
    for chip in range(8):
        begin, count = [], []
        for c in range(2):
            begin.append(start)
            count.append(counts[2 * chip + c])
            start = start + count[c]
        for out, second in ((mine, me == 1), (other, me == 0)):
            first = jnp.where(second, begin[1], begin[0])
            alive = jnp.where(second, count[1], count[0])
            for slot in range(CAP):
                block = order[jnp.minimum(first + slot, 31)]
                ctx = block // 2
                away = jnp.where(ctx % 2 == me, 0, 1024)
                row = away + (ctx // 2) * 128 + (block % 2) * BR
                rows = pl.ds(pl.multiple_of(row, BR), BR)
                keep = jnp.where(slot < alive, 1.0, 0.0).astype(jnp.float32)
                to = pl.ds(slot * BR, BR)
                out[chip, 0, to, :] = (gk[rows, :] * (keep * SCALE)).astype(jnp.bfloat16)
                out[chip, 1, to, :] = (gv[rows, :] * keep).astype(jnp.bfloat16)


def attention_kernel(order, counts, core, kv0, kv1, kv2, q_ref, do_ref, ao_ref, dq, mine, other, gk, gv, kt):
    pieces = [(r, at) for r in (kv0, kv1, kv2) for at in range(0, r.shape[0], CHUNK)]
    spans = [slice(i * CHUNK, (i + 1) * CHUNK) for i in range(len(pieces))]
    keys = lambda i: pieces[i][0][pieces[i][1] : pieces[i][1] + CHUNK, 0:HD]
    values = lambda i: pieces[i][0][pieces[i][1] : pieces[i][1] + CHUNK, HD : 2 * HD]
    every = range(len(pieces))
    for i in every:
        kt[:, spans[i]] = keys(i).T
    for head in range(q_ref.shape[1] // HD):
        cols = slice(head * HD, (head + 1) * HD)
        q, do = q_ref[:, cols], do_ref[:, cols]
        s = [lax.dot_general(keys(i), q, LAST, preferred_element_type=jnp.float32) for i in every]
        top = functools.reduce(jnp.maximum, [x.max(axis=0, keepdims=True) for x in s])
        top = top * (SCALE * LOG2E)
        e = [jnp.exp2(x * (SCALE * LOG2E) - top) for x in s]
        inverse = 1.0 / functools.reduce(jnp.add, [x.sum(axis=0, keepdims=True) for x in e])
        both = do.astype(jnp.float32) * ao_ref[:, cols].astype(jnp.float32)
        delta = jnp.sum(both.T, axis=0, keepdims=True)
        dq_t = None
        for i in every:
            dp = lax.dot_general(values(i), do, LAST, preferred_element_type=jnp.float32)
            p = e[i] * inverse
            ds = (p * (dp - delta)).astype(jnp.bfloat16)
            part = jnp.dot(kt[:, spans[i]], ds, preferred_element_type=jnp.float32)
            dq_t = part if dq_t is None else dq_t + part
            key_part = jnp.dot(ds, q, preferred_element_type=jnp.float32)
            value_part = jnp.dot(p.astype(jnp.bfloat16), do, preferred_element_type=jnp.float32)
            if head == 0:
                gk[spans[i]] = key_part
                gv[spans[i]] = value_part
            else:
                gk[spans[i]] += key_part
                gv[spans[i]] += value_part
        dq[:, cols] = (dq_t * SCALE).T.astype(jnp.bfloat16)
    route(order, counts, core, gk, gv, mine, other)


def attention(order, counts, core, kv_here, kv_there, queries, out_grad, attn_out):
    rows, width = queries.shape
    image = 2 * kv_here.shape[0]
    smem = pl.BlockSpec(memory_space=pltpu.SMEM)
    vmem = pl.BlockSpec(memory_space=pltpu.VMEM)
    grads = jax.ShapeDtypeStruct((8, 2, CAP * BR, HD), jnp.bfloat16)
    return pl.pallas_call(
        attention_kernel,
        in_specs=[smem] * 3 + [vmem] * 6,
        out_specs=[vmem] * 3,
        out_shape=[jax.ShapeDtypeStruct(queries.shape, jnp.bfloat16), grads, grads],
        scratch_shapes=[
            pltpu.VMEM((image, HD), jnp.float32),
            pltpu.VMEM((image, HD), jnp.float32),
            pltpu.VMEM((HD, image), jnp.bfloat16),
        ],
        compiler_params=pltpu.CompilerParams(vmem_limit_bytes=24 << 20),
        cost_estimate=pl.CostEstimate(
            flops=0, transcendentals=0, bytes_accessed=0
        ),
        name="attention",
    )(order, counts, core, kv_here, *kv_there, queries, out_grad, attn_out)


def join_kernel(a, b, c, d, out):
    part = a.shape[0]
    for i, ref in enumerate((a, b, c, d)):
        out[i * part : (i + 1) * part, :] = ref[...]


def join(arrays, flops):
    rows, cols = arrays[0].shape
    vmem = pl.BlockSpec(memory_space=pltpu.VMEM)
    return pl.pallas_call(
        join_kernel,
        in_specs=[vmem] * 4,
        out_specs=vmem,
        out_shape=jax.ShapeDtypeStruct((4 * rows, cols), jnp.bfloat16),
        compiler_params=pltpu.CompilerParams(vmem_limit_bytes=4 << 20),
        cost_estimate=pl.CostEstimate(flops=flops, transcendentals=0, bytes_accessed=1 << 20),
        name="join",
    )(*arrays)


def hold_kernel(*refs):
    for ref, out in zip(refs[:4], refs[4:]):
        out[...] = ref[...]


def hold(arrays):
    vmem = pl.BlockSpec(memory_space=pltpu.VMEM)
    return pl.pallas_call(
        hold_kernel,
        in_specs=[vmem] * 4,
        out_specs=[vmem] * 4,
        out_shape=[jax.ShapeDtypeStruct(a.shape, a.dtype) for a in arrays],
        compiler_params=pltpu.CompilerParams(vmem_limit_bytes=4 << 20),
        cost_estimate=pl.CostEstimate(flops=100 << 30, transcendentals=0, bytes_accessed=2 << 20),
        name="hold",
    )(*arrays)


def product_kernel(at, w0, w1, w2, w3, wp, out):
    part = w0.shape[0] // 4
    total = None
    for kx, w in enumerate((w0, w1, w2, w3)):
        for kz in range(4):
            heads = lax.rem(at[0] + 4 - kz, 4) * 4 + lax.rem(at[1] + 4 - kx, 4)
            cols = pl.ds(pl.multiple_of(heads * part, part), part)
            term = jnp.dot(wp[:, cols], w[kz * part : (kz + 1) * part, :], preferred_element_type=jnp.float32)
            total = term if total is None else total + term
    out[...] = total.astype(jnp.bfloat16)


def weight_product(at, pieces, proj_weight):
    width, model = proj_weight.shape
    vmem = pl.BlockSpec(memory_space=pltpu.VMEM)
    return pl.pallas_call(
        product_kernel,
        in_specs=[pl.BlockSpec(memory_space=pltpu.SMEM)] + [vmem] * 5,
        out_specs=vmem,
        out_shape=jax.ShapeDtypeStruct((width, HD), jnp.bfloat16),
        compiler_params=pltpu.CompilerParams(vmem_limit_bytes=14 << 20),
        cost_estimate=pl.CostEstimate(
            flops=2 * width * model * HD, transcendentals=0, bytes_accessed=10 << 20
        ),
        name="weight_product",
    )(at, *pieces, proj_weight)


def final_kernel(at, heads_at, *refs):
    grads, here, there, out, held = refs[0], refs[1:5], refs[5:9], refs[9], refs[10]
    rows = out.shape[1]
    for x in range(4):
        for kz in range(4):
            heads = lax.rem(heads_at[0] + 4 - kz, 4) * 4 + x
            held[heads] = grads[x, kz * rows : (kz + 1) * rows, :]
    total = None
    for back in range(4):
        for lane in range(2):
            chip = (at[0] ^ lane) * 4 + lax.rem(at[1] + 4 - back, 4)
            term = lax.dot_general(
                jnp.concatenate([here[back][lane], there[back][lane]], axis=1),
                jnp.concatenate([held[2 * chip + at[2]], held[2 * chip + 1 - at[2]]], axis=1),
                LAST,
                preferred_element_type=jnp.float32,
            )
            total = term if total is None else total + term
    out[...] = total.astype(jnp.bfloat16)


def final_product(at, heads_at, grads, here, there):
    rows = grads.shape[1] // 4
    width = here[0].shape[1]
    smem = pl.BlockSpec(memory_space=pltpu.SMEM)
    vmem = pl.BlockSpec(memory_space=pltpu.VMEM)
    return pl.pallas_call(
        final_kernel,
        out_shape=jax.ShapeDtypeStruct((width, rows), jnp.bfloat16),
        in_specs=[smem] * 2 + [vmem] * 9,
        out_specs=vmem,
        scratch_shapes=[pltpu.VMEM((16, rows, HD), jnp.bfloat16)],
        compiler_params=pltpu.CompilerParams(vmem_limit_bytes=16 << 20),
        cost_estimate=pl.CostEstimate(
            flops=2 * rows * width * 2048, transcendentals=0, bytes_accessed=4 << 20
        ),
        name="final_product",
    )(at, heads_at, grads, *here, *there)


def everywhere(array, axes, count):
    copies = jnp.broadcast_to(array, (count, *array.shape))
    return lax.all_to_all(copies, axes, split_axis=0, concat_axis=0, tiled=True)


def swap(axis, array):
    return lax.ppermute(array, axis, [(0, 1), (1, 0)])


def ring(array, axes):
    return [array] + [lax.ppermute(array, axes, [(i, (i + k) % 4) for i in range(4)]) for k in (1, 2, 3)]


def shards(
    queries,
    out_grad,
    attn_out,
    img_keys,
    img_values,
    key_weight,
    value_weight,
    proj_weight,
    block_order,
    owner_counts,
):
    core = lax.axis_index("co")
    chip = lax.axis_index(CHIPS)
    group = lax.axis_index(("zh", "xh"))

    w = jnp.where(
        core == 0,
        lax.dynamic_slice_in_dim(key_weight, chip * HD, HD, 1),
        lax.dynamic_slice_in_dim(value_weight, chip * HD, HD, 1),
    )
    w = join(ring(w, "zh"), 100 << 30)

    own = jnp.concatenate(
        [
            lax.dynamic_slice_in_dim(img_keys, group * HD, HD, 1),
            lax.dynamic_slice_in_dim(img_values, group * HD, HD, 1),
        ],
        axis=1,
    )
    kv = everywhere(own, CHIPS, 8).reshape(1024, 2 * HD)
    w = ring(w, ("xh", "xl"))
    d_query, mine, other = attention(
        block_order, owner_counts, core.reshape(1), kv, [swap("co", kv[:512]), swap("co", kv[512:])], queries, out_grad, attn_out
    )
    other, *w = lax.optimization_barrier((other, *w))
    pair = mine.astype(jnp.float32) + swap("co", other).astype(jnp.float32)
    pair = pair.astype(jnp.bfloat16).reshape(16, CAP * BR, HD)
    pieces = lax.all_to_all(
        pair,
        ("zl", "y", "xl"),
        split_axis=0,
        concat_axis=0,
        tiled=True,
    )
    summed = jnp.sum(pieces.astype(jnp.float32), axis=0).astype(jnp.bfloat16)

    at = jnp.stack([lax.axis_index(a) for a in CTX])
    heads_at = jnp.stack([lax.axis_index("zh"), lax.axis_index(("xh", "xl"))])
    product = weight_product(heads_at, w, proj_weight)
    product = jnp.stack([product, swap("zl", product)])
    summed, product = lax.optimization_barrier((summed, product))
    grads = everywhere(join(ring(summed, "zh"), 30 << 30), X, 4)
    product = hold(ring(product, "y"))
    d_vision = final_product(at, heads_at, grads, product, [swap("co", p) for p in product])
    return (d_query, d_vision.T)


def solution(mesh):
    fine = Mesh(mesh.devices.reshape(2, 4, 2, 4, 2, 2), (*CTX, *HEADS))
    placed = (
        P(CTX, HEADS),
        P(CTX, HEADS),
        P(CTX, HEADS),
        P(CTX, None),
        P(CTX, None),
        P(HEADS, None),
        P(HEADS, None),
        P(HEADS, None),
        P(),
        P(),
    )
    return jax.shard_map(
        shards,
        mesh=fine,
        in_specs=placed,
        out_specs=(P(CTX, HEADS), P(CTX, HEADS)),
        check_vma=False,
    )
```
